32 devices in a mesh: row: 4 (over z), col: 4 (over y, core), depth: 2 (over x).
Axes of the slice: x: 2, y: 2, z: 4, core: 2. Of those that a mesh axis runs over, the one named last changes fastest.
Arguments:
- tokens: bfloat16 [256, 12288], P(('row', 'col'), 'depth'), may hold values from -6 to 6
- in_weight: bfloat16 [12288, 49152], P('depth', ('row', 'col')), may hold values from -0.0546875 to 0.0546875
- in_bias: bfloat16 [49152], P(('row', 'col')), may hold values from -4 to 4
- out_weight: bfloat16 [49152, 12288], P(('row', 'col'), 'depth'), may hold values from -0.02734375 to 0.02734375
- out_bias: bfloat16 [12288], P('depth'), may hold values from -3 to 3
Outputs:
- outputs: bfloat16 [256, 12288], P(('row', 'col'), 'depth')
The draws below stay inside these ranges and needn't reach their ends.
All inputs are finite; a program needn't handle non-finite values.
Results may differ from the reference program's by a relative error of at most 0.0045.
Values may be sent and summed in bfloat16 or wider, within the bound.
A program may use at most 192 MiB of HBM per device.

```python
import jax
import jax.numpy as jnp

D = 12288
FF = 49152
TOKENS = 256


def shard_levels(own_key, extent, split, least, top_value):
    def one(dim, shards_of):
        draws = jax.random.uniform(jax.random.fold_in(jax.random.fold_in(own_key, 6), dim), (shards_of,), jnp.float32, least / len(split), top_value / len(split))
        return jnp.repeat(jnp.exp(draws), extent[dim] // shards_of).reshape((-1,) + (1,) * (len(extent) - dim - 1))

    gain = one(*split[0])
    for cut in split[1:]:
        gain = gain * one(*cut)
    return gain


def scatter_about(rng, shape, width, reach, cuts=(), dtype=jnp.bfloat16):
    gain = shard_levels(rng, shape, cuts, -0.22, 0.18) if cuts else 1.0
    entries = jax.random.normal(rng, shape, jnp.float32) * width * gain
    return jnp.minimum(jnp.maximum(entries, -reach), reach).astype(dtype)


def setup_inputs(seed: int = 0) -> dict:
    keys = jax.random.split(jax.random.key(seed), 6)
    tokens = scatter_about(keys[0], (TOKENS, D), 1.0, 6.0, ((0, 16), (1, 2)))
    in_weight = scatter_about(keys[1], (D, FF), D ** -0.5, 0.0546875, ((0, 2), (1, 16)))
    in_bias = scatter_about(keys[2], (FF,), 1.0, 4.0, ((0, 16),))
    out_weight = scatter_about(keys[3], (FF, D), FF ** -0.5, 0.02734375, ((0, 16), (1, 2)))
    out_bias = scatter_about(keys[4], (D,), 0.5, 3.0, ((0, 2),))
    return {"tokens": tokens, "in_weight": in_weight, "in_bias": in_bias, "out_weight": out_weight, "out_bias": out_bias}


def reference(tokens, in_weight, in_bias, out_weight, out_bias):
    pre = jnp.dot(tokens, in_weight, preferred_element_type=jnp.float32) + in_bias.astype(jnp.float32)
    hidden = jax.nn.gelu(pre, approximate=True).astype(jnp.bfloat16)
    summed = jnp.dot(hidden, out_weight, preferred_element_type=jnp.float32) + out_bias.astype(jnp.float32)
    return summed.astype(jnp.bfloat16)
```

```python
import functools

import jax
import jax.numpy as jnp
from jax import lax
from jax.experimental import pallas as pl
from jax.experimental.pallas import tpu as pltpu
from jax.sharding import PartitionSpec as P

CORES = 2
BF16 = jnp.bfloat16
F32 = jnp.float32


def kernel(
    R, C, DP, tps, nch, nb, ch,
    x_ref, w1_ref, b1_ref, w2_ref, b2_ref, out_ref,
    xbuf, slots, own, psend, precv, hbuf, acc, s1s, s1r, s2s, s2r, own2, s3s, s3r,
    w1_sem, w2_sem, ag_ss, ag_rs, p_ss, p_rs, s1_ss, s1_rs, s2_ss, s2_rs, s3_ss, s3_rs,
):
    Y = C // CORES
    z = lax.axis_index("row")
    col = lax.axis_index("col")
    dp = lax.axis_index("depth")
    y = col // CORES
    c = col % CORES
    sib = y * CORES + (1 - c)

    def remote(src, dst, ss, rs, **dev):
        return pltpu.make_async_remote_copy(
            src_ref=src, dst_ref=dst, send_sem=ss, recv_sem=rs,
            device_id=dev, device_id_type=pl.DeviceIdType.MESH,
        )

    def w1_copy(k):
        return pltpu.make_async_copy(w1_ref.at[:, pl.ds(pl.multiple_of(k * ch, ch), ch)], slots.at[k], w1_sem.at[k])

    def w2_copy(k, n):
        return pltpu.make_async_copy(
            w2_ref.at[pl.ds(pl.multiple_of(k * ch, ch), ch), pl.ds(pl.multiple_of(n * ch, ch), ch)],
            slots.at[k, pl.ds(pl.multiple_of(n * ch, ch), ch)],
            w2_sem.at[k, n],
        )

    @pl.loop(0, nch)
    def _(k):
        w1_copy(k).start()

    barrier = pltpu.get_barrier_semaphore()

    def greet(**dev):
        pl.semaphore_signal(barrier, inc=1, device_id=dev, device_id_type=pl.DeviceIdType.MESH)

    z_peers = [(z + dz) % R for dz in range(1, R)]
    y_peers = [(y + dy) % Y for dy in range(1, Y)]
    d_peers = [(dp + dd) % DP for dd in range(1, DP)]
    for zt in z_peers:
        greet(row=zt)
    for yt in y_peers:
        greet(col=yt * CORES + c)
    greet(col=sib)
    for dt in d_peers:
        greet(depth=dt)

    def shard(zz, yy, cc):
        return zz * C + yy * CORES + cc

    def rows(s):
        return pl.ds(pl.multiple_of(s * tps, tps), tps)

    me = shard(z, y, c)
    xbuf[rows(me)] = x_ref[...]
    pl.semaphore_wait(barrier, (R - 1) + (Y - 1) + 1 + (DP - 1))

    sent = []

    def send_shard(s, **dev):
        copy = remote(xbuf.at[rows(s)], xbuf.at[rows(s)], ag_ss.at[len(sent)], ag_rs.at[s], **dev)
        copy.start()
        sent.append(copy)

    def await_shard(s):
        remote(xbuf.at[rows(s)], xbuf.at[rows(s)], ag_ss.at[0], ag_rs.at[s], col=sib).wait_recv()

    for zt in z_peers:
        send_shard(me, row=zt)
    for yt in y_peers:
        send_shard(me, col=yt * CORES + c)
    send_shard(me, col=sib)

    @pl.loop(0, nb)
    def _(n):
        acc[n] = jnp.zeros(acc.shape[1:], F32)

    for zt in z_peers:
        s = shard(zt, y, c)
        await_shard(s)
        for yt in y_peers:
            send_shard(s, col=yt * CORES + c)
        send_shard(s, col=sib)
    for yt in y_peers:
        for zt in [z] + z_peers:
            s = shard(zt, yt, c)
            await_shard(s)
            send_shard(s, col=sib)
    for yt in [y] + y_peers:
        for zt in [z] + z_peers:
            await_shard(shard(zt, yt, 1 - c))

    def p_copy(i, k):
        return remote(psend.at[k], precv.at[i, k], p_ss.at[i, k], p_rs.at[i, k], depth=d_peers[i])

    @pl.loop(0, nch)
    def _(k):
        w1_copy(k).wait()
        partial = jnp.dot(xbuf[...], slots[k], preferred_element_type=F32)
        own[k] = partial
        psend[k] = partial.astype(BF16)
        for i in range(DP - 1):
            p_copy(i, k).start()

        @pl.loop(0, nb)
        def _(n):
            w2_copy(k, n).start()

    def hidden(k):
        for i in range(DP - 1):
            p_copy(i, k).wait_recv()
        pre = own[k]
        for i in range(DP - 1):
            pre = pre + precv[i, k].astype(F32)
        pre = pre + b1_ref[:, pl.ds(pl.multiple_of(k * ch, ch), ch)].astype(F32)
        hbuf[...] = jax.nn.gelu(pre, approximate=True).astype(BF16)

    def accumulate(k, n):
        w2_copy(k, n).wait()
        acc[n] += jnp.dot(
            hbuf[...], slots[k, pl.ds(pl.multiple_of(n * ch, ch), ch)], preferred_element_type=F32
        )

    @pl.loop(0, nch - 1)
    def _(k):
        hidden(k)

        @pl.loop(0, nb)
        def _(n):
            accumulate(k, n)

    def s1_copy(n):
        return remote(s1s.at[n], s1r.at[n], s1_ss.at[n], s1_rs.at[n], col=sib)

    def s2_copy(i, n):
        return remote(s2s.at[i, n], s2r.at[i, n], s2_ss.at[i, n], s2_rs.at[i, n], col=y_peers[i] * CORES + c)

    def s3_copy(i, n):
        return remote(s3s.at[i, n], s3r.at[i, n], s3_ss.at[i, n], s3_rs.at[i, n], row=z_peers[i])

    def stage2(n):
        s1_copy(n).wait_recv()

        def chip_sum(j):
            return acc[n, rows(CORES * j + c)] + s1r[n, rows(j)].astype(F32)

        for i, yt in enumerate(y_peers):
            for zz in range(R):
                s2s[i, n, rows(zz)] = chip_sum(zz * Y + yt).astype(BF16)
            s2_copy(i, n).start()
        for zz in range(R):
            own2[n, rows(zz)] = chip_sum(zz * Y + y)

    hidden(nch - 1)

    @pl.loop(0, nb)
    def _(n):
        accumulate(nch - 1, n)
        for j in range(R * Y):
            s1s[n, rows(j)] = acc[n, rows(CORES * j + 1 - c)].astype(BF16)
        s1_copy(n).start()

        @pl.when(n > 0)
        def _():
            stage2(n - 1)

    stage2(nb - 1)

    @pl.loop(0, nb)
    def _(n):
        total = own2[n]
        for i in range(Y - 1):
            s2_copy(i, n).wait_recv()
        for i in range(Y - 1):
            total = total + s2r[i, n].astype(F32)
        own2[n] = total
        for i, zt in enumerate(z_peers):
            s3s[i, n] = own2[n, rows(zt)].astype(BF16)
            s3_copy(i, n).start()

    @pl.loop(0, nb)
    def _(n):
        cols = pl.ds(pl.multiple_of(n * ch, ch), ch)
        for i in range(R - 1):
            s3_copy(i, n).wait_recv()
        total = own2[n, rows(z)]
        for i in range(R - 1):
            total = total + s3r[i, n].astype(F32)
        out_ref[:, cols] = (total + b2_ref[:, cols].astype(F32)).astype(BF16)

    for copy in sent:
        copy.wait_send()

    @pl.loop(0, nch)
    def _(k):
        for i in range(DP - 1):
            p_copy(i, k).wait_send()

    @pl.loop(0, nb)
    def _(n):
        s1_copy(n).wait_send()
        for i in range(Y - 1):
            s2_copy(i, n).wait_send()
        for i in range(R - 1):
            s3_copy(i, n).wait_send()


def solution(mesh):
    R, C, DP = mesh.shape["row"], mesh.shape["col"], mesh.shape["depth"]
    Y = C // CORES

    def body(tokens, in_weight, in_bias, out_weight, out_bias):
        tps, dl = tokens.shape
        ffl = in_weight.shape[1]
        T = tps * R * C
        ch = 512
        nch, nb = ffl // ch, dl // ch
        n_ag = (R - 1) + (Y - 1) + 1 + (R - 1) * Y + (Y - 1) * R
        vmem = pl.BlockSpec(memory_space=pltpu.VMEM)
        hbm = pl.BlockSpec(memory_space=pl.ANY)
        dma = pltpu.SemaphoreType.DMA
        return pl.pallas_call(
            functools.partial(kernel, R, C, DP, tps, nch, nb, ch),
            out_shape=jax.ShapeDtypeStruct((tps, dl), BF16),
            in_specs=[vmem, hbm, vmem, hbm, vmem],
            out_specs=vmem,
            scratch_shapes=[
                pltpu.VMEM((T, dl), BF16),
                pltpu.VMEM((nch, dl, ch), BF16),
                pltpu.VMEM((nch, T, ch), F32),
                pltpu.VMEM((nch, T, ch), BF16),
                pltpu.VMEM((DP - 1, nch, T, ch), BF16),
                pltpu.VMEM((T, ch), BF16),
                pltpu.VMEM((nb, T, ch), F32),
                pltpu.VMEM((nb, T // CORES, ch), BF16),
                pltpu.VMEM((nb, T // CORES, ch), BF16),
                pltpu.VMEM((Y - 1, nb, R * tps, ch), BF16),
                pltpu.VMEM((Y - 1, nb, R * tps, ch), BF16),
                pltpu.VMEM((nb, R * tps, ch), F32),
                pltpu.VMEM((R - 1, nb, tps, ch), BF16),
                pltpu.VMEM((R - 1, nb, tps, ch), BF16),
                dma((nch,)),
                dma((nch, nb)),
                dma((n_ag,)),
                dma((R * C,)),
                dma((DP - 1, nch)),
                dma((DP - 1, nch)),
                dma((nb,)),
                dma((nb,)),
                dma((Y - 1, nb)),
                dma((Y - 1, nb)),
                dma((R - 1, nb)),
                dma((R - 1, nb)),
            ],
            compiler_params=pltpu.CompilerParams(
                collective_id=0, has_side_effects=True, vmem_limit_bytes=63 * 1024 * 1024
            ),
        )(tokens, in_weight, in_bias.reshape(1, ffl), out_weight, out_bias.reshape(1, dl))

    in_specs = (
        P(("row", "col"), "depth"),
        P("depth", ("row", "col")),
        P(("row", "col")),
        P(("row", "col"), "depth"),
        P("depth"),
    )
    out_specs = P(("row", "col"), "depth")
    return jax.shard_map(body, mesh=mesh, in_specs=in_specs, out_specs=out_specs, check_vma=False)
```

```python
import functools

import jax
import jax.numpy as jnp
from jax import lax
from jax.experimental import pallas as pl
from jax.experimental.pallas import tpu as pltpu
from jax.sharding import PartitionSpec as P

CORES = 2
BF16 = jnp.bfloat16
F32 = jnp.float32


def partner(i, step, n):
    if n & (n - 1):
        return (i + step) % n
    out, bit = 0, 1
    while bit < n:
        own = i // bit % 2
        out = out + bit * (1 - own if step & bit else own)
        bit *= 2
    return out


def kernel(
    R, C, DP, tps, nch, nb, ch,
    x_ref, w1_ref, b1_ref, w2_ref, b2_ref, out_ref,
    xbuf, slots, own, psend, precv, hbuf, acc, s1s, s1r, s2s, s2r, own2, s3s, s3r,
    w1_sem, w2_sem, ag_ss, ag_rs, p_ss, p_rs, s1_ss, s1_rs, s2_ss, s2_rs, s3_ss, s3_rs,
):
    Y = C // CORES
    z = lax.axis_index("row")
    col = lax.axis_index("col")
    dp = lax.axis_index("depth")
    y = col // CORES
    c = col % CORES
    sib = y * CORES + (1 - c)

    def remote(src, dst, ss, rs, **dev):
        return pltpu.make_async_remote_copy(
            src_ref=src, dst_ref=dst, send_sem=ss, recv_sem=rs,
            device_id=dev, device_id_type=pl.DeviceIdType.MESH,
        )

    def w1_copy(k):
        return pltpu.make_async_copy(w1_ref.at[:, pl.ds(pl.multiple_of(k * ch, ch), ch)], slots.at[k], w1_sem.at[k])

    ffl = w2_ref.shape[0]
    per = nb // nch

    def w2_slot(n):
        return n // per, pl.ds(pl.multiple_of(n % per * ffl, ffl), ffl)

    def w2_copy(n):
        return pltpu.make_async_copy(
            w2_ref.at[:, pl.ds(pl.multiple_of(n * ch, ch), ch)], slots.at[w2_slot(n)], w2_sem.at[n]
        )

    @pl.loop(0, nch)
    def _(k):
        w1_copy(k).start()

    barrier = pltpu.get_barrier_semaphore()

    def greet(**dev):
        pl.semaphore_signal(barrier, inc=1, device_id=dev, device_id_type=pl.DeviceIdType.MESH)

    z_peers = [partner(z, dz, R) for dz in range(1, R)]
    chain = R == 4
    far = 1 - z // (R // 2)
    if chain:
        z_order = [z, partner(z, 1, R), 1 + far, 3 * far]
        across = 3 - z
        inner = (z == 1) | (z == 2)
    else:
        z_order = [z] + z_peers
    y_peers = [(y + dy) % Y for dy in range(1, Y)]
    d_peers = [(dp + dd) % DP for dd in range(1, DP)]
    for zt in z_peers:
        greet(row=zt)
    for yt in y_peers:
        greet(col=yt * CORES + c)
    greet(col=sib)
    for dt in d_peers:
        greet(depth=dt)

    def shard(zz, yy, cc):
        return zz * C + yy * CORES + cc

    def rows(s):
        return pl.ds(pl.multiple_of(s * tps, tps), tps)

    me = shard(z, y, c)
    xbuf[rows(me)] = x_ref[...]
    pl.semaphore_wait(barrier, (R - 1) + (Y - 1) + 1 + (DP - 1))

    sent = []

    def send_shard(s, inner_only=False, **dev):
        copy = remote(xbuf.at[rows(s)], xbuf.at[rows(s)], ag_ss.at[len(sent)], ag_rs.at[s], **dev)
        sent.append((copy, inner_only))
        if inner_only:
            pl.when(inner)(copy.start)
        else:
            copy.start()

    def await_shard(s):
        remote(xbuf.at[rows(s)], xbuf.at[rows(s)], ag_ss.at[0], ag_rs.at[s], col=sib).wait_recv()

    if chain:
        send_shard(me, inner_only=True, row=across)
        send_shard(me, row=z_order[1])
    else:
        for zt in z_peers:
            send_shard(me, row=zt)
    for yt in y_peers:
        send_shard(me, col=yt * CORES + c)
    send_shard(me, col=sib)

    def forward_z(i):
        s = shard(z_order[i], y, c)
        await_shard(s)
        if chain:
            send_shard(s, inner_only=True, row=across if i == 1 else z_order[1])
        for yt in y_peers:
            send_shard(s, col=yt * CORES + c)
        send_shard(s, col=sib)

    def forward_y(i):
        for yt in y_peers:
            s = shard(z_order[i], yt, c)
            await_shard(s)
            send_shard(s, col=sib)

    half = R // 2

    def block_rows(b):
        size = half * C * tps
        return pl.ds(pl.multiple_of((1 - far if b == 0 else far) * size, size), size)

    def p_copy(i, k, b):
        r = block_rows(b)
        return remote(
            psend.at[k, r], precv.at[i, k, r], p_ss.at[i, k, b], p_rs.at[i, k, b], depth=d_peers[i]
        )

    def project(b, first, last):
        r = block_rows(b)

        @pl.loop(first, last)
        def _(k):
            if b == 0:
                w1_copy(k).wait()
            partial = jnp.dot(xbuf[r], slots[k], preferred_element_type=F32)
            own[k, r] = partial
            psend[k, r] = partial.astype(BF16)
            for i in range(DP - 1):
                p_copy(i, k, b).start()
            if b == 1:
                for j in range(per):
                    w2_copy(k * per + j).start()

    def await_block(b):
        for i in range(b * half, (b + 1) * half):
            for yt in [y] + y_peers:
                await_shard(shard(z_order[i], yt, 1 - c))

    for i in range(1, half):
        forward_z(i)
    for i in range(half):
        forward_y(i)
    forward_z(half)
    await_block(0)
    cut1, cut2 = nch // 3, 2 * nch // 3
    project(0, 0, cut1)
    for i in range(half + 1, R):
        forward_z(i)
    forward_y(half)
    project(0, cut1, cut2)
    for i in range(half + 1, R):
        forward_y(i)
    project(0, cut2, nch)
    await_block(1)
    project(1, 0, nch)

    def hidden(k):
        for i in range(DP - 1):
            for b in range(2):
                p_copy(i, k, b).wait_recv()
        pre = own[k]
        for i in range(DP - 1):
            pre = pre + precv[i, k].astype(F32)
        cols = pl.ds(pl.multiple_of(k * ch, ch), ch)
        pre = pre + b1_ref[:, cols].astype(F32)
        hbuf[:, cols] = jax.nn.gelu(pre, approximate=True).astype(BF16)

    def multiply(n):
        w2_copy(n).wait()
        acc[n] = jnp.dot(hbuf[...], slots[w2_slot(n)], preferred_element_type=F32)

    pl.loop(0, nch)(hidden)

    def s1_copy(n):
        return remote(s1s.at[n], s1r.at[n], s1_ss.at[n], s1_rs.at[n], col=sib)

    def s2_copy(i, n):
        return remote(s2s.at[i, n], s2r.at[i, n], s2_ss.at[i, n], s2_rs.at[i, n], col=y_peers[i] * CORES + c)

    def s3_copy(i, n):
        return remote(s3s.at[i, n], s3r.at[i, n], s3_ss.at[i, n], s3_rs.at[i, n], row=z_peers[i])

    def stage2(n):
        s1_copy(n).wait_recv()

        def chip_sum(j):
            return acc[n, rows(CORES * j + c)] + s1r[n, rows(j)].astype(F32)

        for i, yt in enumerate(y_peers):
            for zz in range(R):
                s2s[i, n, rows(zz)] = chip_sum(zz * Y + yt).astype(BF16)
            s2_copy(i, n).start()
        for zz in range(R):
            own2[n, rows(zz)] = chip_sum(zz * Y + y)

    @pl.loop(0, nb)
    def _(n):
        multiply(n)
        for j in range(R * Y):
            s1s[n, rows(j)] = acc[n, rows(CORES * j + 1 - c)].astype(BF16)
        s1_copy(n).start()

        @pl.when(n > 0)
        def _():
            stage2(n - 1)

    stage2(nb - 1)

    @pl.loop(0, nb)
    def _(n):
        total = own2[n]
        for i in range(Y - 1):
            s2_copy(i, n).wait_recv()
        for i in range(Y - 1):
            total = total + s2r[i, n].astype(F32)
        own2[n] = total
        for i, zt in enumerate(z_peers):
            s3s[i, n] = own2[n, rows(zt)].astype(BF16)
            s3_copy(i, n).start()

    @pl.loop(0, nb)
    def _(n):
        cols = pl.ds(pl.multiple_of(n * ch, ch), ch)
        for i in range(R - 1):
            s3_copy(i, n).wait_recv()
        total = own2[n, rows(z)]
        for i in range(R - 1):
            total = total + s3r[i, n].astype(F32)
        out_ref[:, cols] = (total + b2_ref[:, cols].astype(F32)).astype(BF16)

    for copy, inner_only in sent:
        if inner_only:
            pl.when(inner)(copy.wait_send)
        else:
            copy.wait_send()

    @pl.loop(0, nch)
    def _(k):
        for i in range(DP - 1):
            for b in range(2):
                p_copy(i, k, b).wait_send()

    @pl.loop(0, nb)
    def _(n):
        s1_copy(n).wait_send()
        for i in range(Y - 1):
            s2_copy(i, n).wait_send()
        for i in range(R - 1):
            s3_copy(i, n).wait_send()


def solution(mesh):
    R, C, DP = mesh.shape["row"], mesh.shape["col"], mesh.shape["depth"]
    Y = C // CORES

    def body(tokens, in_weight, in_bias, out_weight, out_bias):
        tps, dl = tokens.shape
        ffl = in_weight.shape[1]
        T = tps * R * C
        ch = 512
        nch, nb = ffl // ch, dl // ch
        n_ag = 3 * R * Y + R
        vmem = pl.BlockSpec(memory_space=pltpu.VMEM)
        hbm = pl.BlockSpec(memory_space=pl.ANY)
        dma = pltpu.SemaphoreType.DMA
        return pl.pallas_call(
            functools.partial(kernel, R, C, DP, tps, nch, nb, ch),
            out_shape=jax.ShapeDtypeStruct((tps, dl), BF16),
            in_specs=[vmem, hbm, vmem, hbm, vmem],
            out_specs=vmem,
            scratch_shapes=[
                pltpu.VMEM((T, dl), BF16),
                pltpu.VMEM((nch, dl, ch), BF16),
                pltpu.VMEM((nch, T, ch), F32),
                pltpu.VMEM((nch, T, ch), BF16),
                pltpu.VMEM((DP - 1, nch, T, ch), BF16),
                pltpu.VMEM((T, ffl), BF16),
                pltpu.VMEM((nb, T, ch), F32),
                pltpu.VMEM((nb, T // CORES, ch), BF16),
                pltpu.VMEM((nb, T // CORES, ch), BF16),
                pltpu.VMEM((Y - 1, nb, R * tps, ch), BF16),
                pltpu.VMEM((Y - 1, nb, R * tps, ch), BF16),
                pltpu.VMEM((nb, R * tps, ch), F32),
                pltpu.VMEM((R - 1, nb, tps, ch), BF16),
                pltpu.VMEM((R - 1, nb, tps, ch), BF16),
                dma((nch,)),
                dma((nb,)),
                dma((n_ag,)),
                dma((R * C,)),
                dma((DP - 1, nch, 2)),
                dma((DP - 1, nch, 2)),
                dma((nb,)),
                dma((nb,)),
                dma((Y - 1, nb)),
                dma((Y - 1, nb)),
                dma((R - 1, nb)),
                dma((R - 1, nb)),
            ],
            compiler_params=pltpu.CompilerParams(
                collective_id=0, has_side_effects=True, vmem_limit_bytes=63 * 1024 * 1024
            ),
        )(tokens, in_weight, in_bias.reshape(1, ffl), out_weight, out_bias.reshape(1, dl))

    in_specs = (
        P(("row", "col"), "depth"),
        P("depth", ("row", "col")),
        P(("row", "col")),
        P(("row", "col"), "depth"),
        P("depth"),
    )
    out_specs = P(("row", "col"), "depth")
    return jax.shard_map(body, mesh=mesh, in_specs=in_specs, out_specs=out_specs, check_vma=False)
```
